512 devices in a mesh: row: 8 (over z_lo, x), col: 16 (over y, core), freq: 4 (over z_hi).
Axes of the slice: x: 4, y: 8, z: 8 (z_hi: 4, z_lo: 2; z = z_hi * 2 + z_lo), core: 2. Of those that a mesh axis runs over, the one named last changes fastest.
Arguments:
- covariance: bfloat16 [16, 2, 4096, 4096], P('freq', None, 'row', 'col'), may hold values from -30 to 30, as said below
- replica_table: bfloat16 [16, 2, 4096, 512], P('freq', None, 'col'), may hold values from -18 to 18
- slab_index: int32 [384], replicated, may hold values from 0 to 511
Outputs:
- power: float32 [16, 384], P('freq', ('row', 'col'))
- surface: float32 [384], P(('row', 'col'))
The draws below stay inside these ranges and needn't reach their ends.
Inputs may be any that keep to these rules, and one draw needn't show every extreme that they name: For each frequency, covariance is Hermitian: its real part is symmetric and its imaginary part antisymmetric, and the whole is positive definite.
All inputs are finite; a program needn't handle non-finite values.
Results may differ from the reference program's by a relative error of at most 0.0003.
Values may be sent and summed in bfloat16 or wider, within the bound.
A program may use at most 64 MiB of HBM per device.

```python
import math
import jax
import jax.numpy as jnp
from jax import lax

CH = 4096
FREQ = 16
SLAB = 384
TABLE = 512


noise_floor = 0.6


coupling = 0.1


sources = 8


def draw_covariance(key, part):
    spread = coupling / math.sqrt(CH)

    def one_frequency(index):
        subkey = jax.random.fold_in(key, index)
        key_sym = jax.random.fold_in(subkey, 0)
        key_anti = jax.random.fold_in(subkey, 1)
        key_gain = jax.random.fold_in(subkey, 2)
        key_phase = jax.random.fold_in(subkey, 3)
        key_power = jax.random.fold_in(subkey, 5)
        symmetric = jax.random.normal(key_sym, (CH, CH), jnp.float32)
        antisym = jax.random.normal(key_anti, (CH, CH), jnp.float32)
        gains = jnp.exp(jax.random.uniform(key_gain, (CH,), jnp.float32, 0.0, math.log(100.0))) / 10.0
        strength = jnp.exp(jax.random.uniform(key_power, (sources,), jnp.float32, math.log(0.03), math.log(0.25)))
        phase = jax.random.uniform(key_phase, (CH, sources), jnp.float32, -math.pi, math.pi)
        root_power = jnp.sqrt(strength)[None, :]
        cosine = jnp.cos(phase) * root_power
        sine = jnp.sin(phase) * root_power
        source_real = jnp.dot(cosine, cosine.T) + jnp.dot(sine, sine.T)
        source_imag = jnp.dot(sine, cosine.T) - jnp.dot(cosine, sine.T)
        scales = jnp.sqrt(gains)
        outer = scales[:, None] * scales[None, :]
        real_part = (noise_floor * jnp.eye(CH, dtype=jnp.float32) + spread * (symmetric + symmetric.T) + source_real) * outer
        imag_part = (spread * (antisym - antisym.T) + source_imag) * outer
        return jnp.stack([real_part, imag_part]).astype(jnp.bfloat16)
    return lax.map(one_frequency, jnp.arange(FREQ))


def draw_replica_table(key, part):
    key_amp, key_phase = jax.random.split(jax.random.fold_in(key, 7))
    channel = jnp.arange(CH).astype(jnp.float32) / CH
    rising = 3.0 ** channel
    amplitude = jnp.exp(jax.random.uniform(key_amp, (FREQ, CH, TABLE), jnp.float32, math.log(0.5), math.log(2.0)))
    magnitude = amplitude * rising[None, :, None]
    phase = jax.random.uniform(key_phase, (FREQ, CH, TABLE), jnp.float32, -math.pi, math.pi)
    return jnp.stack([magnitude * jnp.cos(phase), magnitude * jnp.sin(phase)], axis=1).astype(jnp.bfloat16)


def touch_ends(values, own_key, low, largest):
    extent = values.shape
    place = [jax.random.randint(jax.random.fold_in(own_key, axis), (), 0, extent[axis]) for axis in range(len(extent))]
    values = values.at[tuple(place)].set(low)
    longest = extent.index(max(extent))
    place[longest] = (place[longest] + 1) % extent[longest]
    return values.at[tuple(place)].set(largest)


def setup_inputs(seed: int = 0) -> dict:
    arg_keys = jax.random.split(jax.random.key(seed), 4)
    covariance = draw_covariance(jax.random.fold_in(arg_keys[3], 71), 0)
    replica_table = draw_replica_table(jax.random.fold_in(arg_keys[3], 71), 0)
    slab_index = touch_ends(jax.random.randint(arg_keys[2], (SLAB,), 0, TABLE), jax.random.fold_in(arg_keys[2], 1), 0, TABLE - 1).astype(jnp.int32)
    return dict(covariance=covariance, replica_table=replica_table, slab_index=slab_index)


def reference(covariance, replica_table, slab_index):
    def one_frequency(index):
        matrix = covariance[index]
        table = replica_table[index]
        replica = jnp.take(table, slab_index, axis=2)
        part_a = replica[0]
        part_b = replica[1]
        real_a = jnp.dot(matrix[0], part_a, preferred_element_type=jnp.float32)
        real_b = jnp.dot(matrix[0], part_b, preferred_element_type=jnp.float32)
        imag_a = jnp.dot(matrix[1], part_a, preferred_element_type=jnp.float32)
        imag_b = jnp.dot(matrix[1], part_b, preferred_element_type=jnp.float32)
        image_real = real_a - imag_b
        image_imag = real_b + imag_a
        wide_a = part_a.astype(jnp.float32)
        wide_b = part_b.astype(jnp.float32)
        quad = jnp.sum(wide_a * image_real + wide_b * image_imag, axis=0)
        weight = jnp.sum(wide_a * wide_a + wide_b * wide_b, axis=0)
        return quad / weight

    power = lax.map(one_frequency, jnp.arange(FREQ))
    surface = jnp.sum(power, axis=0) / FREQ
    return power, surface
```

```python
import functools

import jax
import jax.numpy as jnp
from jax import lax
from jax.experimental import pallas as pl
from jax.experimental.pallas import tpu as pltpu
from jax.sharding import PartitionSpec as P

MESH = pl.DeviceIdType.MESH
F32 = jnp.float32
BF16 = jnp.bfloat16
NCH = 16


def kernel(sizes, cov, tbl, idx, pow_ref, surf_ref,
           T, C, X, OH, IM, B, S, ACC, WT, R1, R2, R3,
           tsem, csem, b_recv, s_recv, up_send, dn_send, z_send, s_send,
           r1_send, r1_recv, r2_send, r2_recv, r3_send, r3_recv):
    n_row, n_col, n_freq, ch, slab, table, total_freqs = sizes
    cr = ch // NCH
    r = lax.axis_index("row")
    c = lax.axis_index("col")
    q = lax.axis_index("freq")
    y = c // 2
    k = c % 2
    zl = r // 4
    d = (y - r + 8) % 8
    up = (r, (c + 2) % 16, q)
    down = (r, (c + 14) % 16, q)
    mate = ((r + 4) % 8, c, q)
    sib = (r, c + 1 - 2 * k, q)

    barrier = pltpu.get_barrier_semaphore()
    for j in range(1, n_col):
        pl.semaphore_signal(barrier, inc=1, device_id=(r, (c + j) % n_col, q), device_id_type=MESH)
    for j in range(1, n_row):
        pl.semaphore_signal(barrier, inc=1, device_id=((r + j) % n_row, c, q), device_id_type=MESH)
    for j in range(1, n_freq):
        pl.semaphore_signal(barrier, inc=1, device_id=(r, c, (q + j) % n_freq), device_id_type=MESH)

    ends = (d == 0) | (d == 4)
    base = jnp.where(d >= 5, 2, 0)
    n_slots = jnp.where(d == 0, 4, 2)

    def freq_of(i):
        first = jnp.where(i == 0, base + zl, jnp.where(ends, 2 + zl, base + 1 - zl))
        return jnp.where(i < 2, first, jnp.where(i == 2, 1 - zl, 3 - zl))

    def table_copy(i):
        return pltpu.make_async_copy(tbl.at[freq_of(i)], T.at[i], tsem.at[i])

    def cov_copies(i):
        out = []
        for part in range(2):
            for half in range(2):
                rows = pl.ds(pl.multiple_of((k if half == 0 else 1 - k) * ch, ch), ch)
                out.append(pltpu.make_async_copy(
                    cov.at[freq_of(i), part, rows, :],
                    C.at[i, pl.ds(half * ch, ch), pl.ds(part * ch, ch)],
                    csem.at[i, 2 * part + half]))
        return out

    def start_table(i, carry):
        table_copy(i).start()
        return carry

    def start_cov(i, carry):
        for copy in cov_copies(i):
            copy.start()
        return carry

    lax.fori_loop(0, n_slots, start_table, 0)
    lax.fori_loop(0, n_slots, start_cov, 0)

    points = lax.broadcasted_iota(jnp.int32, (table, slab), 0)
    OH[...] = jnp.where(points == idx[...], 1.0, 0.0).astype(BF16)
    ACC[...] = jnp.zeros_like(ACC)
    WT[...] = jnp.zeros_like(WT)

    def chunk(j):
        return pl.ds(pl.multiple_of(j * cr, cr), cr)

    def remote(src, dst, send, recv, to):
        return pltpu.make_async_remote_copy(
            src_ref=src, dst_ref=dst, send_sem=send, recv_sem=recv, device_id=to, device_id_type=MESH)

    to_up = jnp.where(d <= 3, 0, 2)
    to_down = jnp.where((d == 0) | (d >= 6), 0, jnp.where(d == 5, 1, 2))
    from_down = jnp.where(d <= 4, 0, 2)
    from_up = jnp.where(d >= 5, 0, jnp.where(d == 4, 1, 2))

    def send_up(src, j):
        return remote(src, B.at[to_up, chunk(j)], up_send, b_recv.at[to_up, j], up)

    def send_down(src, j):
        return remote(src, B.at[to_down, chunk(j)], dn_send, b_recv.at[to_down, j], down)

    def send_mate(src, j):
        return remote(src, B.at[1, chunk(j)], z_send, b_recv.at[1, j], mate)

    def send_sib(src, i, j):
        return remote(src, S.at[i, chunk(j)], s_send.at[i], s_recv.at[i, j], sib)

    def own_rows(i, j):
        return X.at[i, chunk(j), :]

    def gather(i, carry):
        table_copy(i).wait()
        both = jnp.dot(T[i].reshape(2 * ch, table), OH[...], preferred_element_type=F32)
        a, b = both[:ch], both[ch:]
        na, nb = a.astype(BF16), b.astype(BF16)
        X[i, 0:ch, 0:slab] = na
        X[i, 0:ch, slab:2 * slab] = nb
        X[i, ch:2 * ch, 0:slab] = -nb
        X[i, ch:2 * ch, slab:2 * slab] = na

        @pl.when(d == 0)
        def _():
            WT[i] = jnp.sum((a * a + b * b).reshape(ch // 8, 8, slab), axis=0)

        @pl.when(i == 0)
        def _():
            pl.semaphore_wait(barrier, n_col + n_row + n_freq - 3)

        @pl.when(ends & (i == 0))
        def _():
            def go(j, carry):
                send_up(own_rows(i, j), j).start()
                return carry
            lax.fori_loop(0, NCH, go, 0)

        @pl.when(ends & (i == 1))
        def _():
            def go(j, carry):
                send_down(own_rows(i, j), j).start()
                return carry
            lax.fori_loop(0, NCH, go, 0)

        @pl.when(d == 0)
        def _():
            def go(j, carry):
                send_sib(own_rows(i, j), i, j).start()
                return carry
            lax.fori_loop(0, NCH, go, 0)

        return carry

    lax.fori_loop(0, n_slots, gather, 0)

    def image(i, carry):
        for copy in cov_copies(i):
            copy.wait()
        IM[i] = jnp.dot(C[i], X[i], preferred_element_type=F32)
        return carry

    lax.fori_loop(0, n_slots, image, 0)

    def wait_in(slot, j):
        remote(B.at[slot, chunk(j)], B.at[slot, chunk(j)], z_send, b_recv.at[slot, j], sib).wait_recv()

    def wait_sib(i, j):
        remote(S.at[i, chunk(j)], S.at[i, chunk(j)], z_send, s_recv.at[i, j], sib).wait_recv()

    def fold(w, im):
        return jnp.sum((w.astype(F32) * im).reshape(cr // 8, 8, 2 * slab), axis=0)

    def combine(own, i, j):
        mine = fold(own[...], IM[i, chunk(j), :])
        other = pl.ds(pl.multiple_of(ch + j * cr, cr), cr)
        ACC[i] += mine + fold(S[i, chunk(j), :], IM[i, other, :])

    @pl.when(d == 0)
    def _():
        def each(m, carry):
            i, j = m // NCH, m % NCH
            wait_sib(i, j)
            combine(own_rows(i, j), i, j)
            return carry
        lax.fori_loop(0, 4 * NCH, each, 0)

    hops = jnp.where(d <= 4, d, 8 - d)

    @pl.when(d != 0)
    def _():
        lag_p = jnp.where(d <= 4, d, d - 4) - 1
        lag_m = jnp.where(d >= 4, 8 - d, 4 - d) - 1
        lag_1 = jnp.where(d == 4, 4, hops + 1)

        def within(j):
            return (j >= 0) & (j < NCH)

        def step(t, carry):
            jp = t - lag_p

            @pl.when(within(jp))
            def _():
                wait_in(from_down, jp)
                here = B.at[from_down, chunk(jp)]

                @pl.when((d != 4) & (d != 7))
                def _():
                    send_up(here, jp).start()

                @pl.when(d <= 4)
                def _():
                    send_sib(here, 0, jp).start()

                @pl.when(d >= 5)
                def _():
                    send_mate(here, jp).start()

            jm = t - lag_m

            @pl.when(within(jm))
            def _():
                wait_in(from_up, jm)
                here = B.at[from_up, chunk(jm)]

                @pl.when((d != 4) & (d != 1))
                def _():
                    send_down(here, jm).start()

                @pl.when(d >= 4)
                def _():
                    send_sib(here, from_up, jm).start()

                @pl.when(d <= 3)
                def _():
                    send_mate(here, jm).start()

            jz = t - hops

            @pl.when(within(jz) & (d != 4))
            def _():
                wait_in(1, jz)
                send_sib(B.at[1, chunk(jz)], 1, jz).start()

            j0 = t - hops

            @pl.when(within(j0))
            def _():
                wait_sib(0, j0)
                combine(B.at[0, chunk(j0)], 0, j0)

            j1 = t - lag_1

            @pl.when(within(j1))
            def _():
                wait_sib(1, j1)
                combine(B.at[1, chunk(j1)], 1, j1)

            return carry

        lax.fori_loop(0, NCH + 4, step, 0)

    scale = jnp.where(d == 0, 1.0, 2.0).astype(F32)
    rows8 = lax.broadcasted_iota(jnp.int32, (8, slab), 0)
    part = jnp.zeros((8, slab), F32)
    for i in range(4):
        live = i < n_slots
        sums = (ACC[i, :, 0:slab] + ACC[i, :, slab:2 * slab]) * scale
        quad = jnp.sum(sums, axis=0, keepdims=True)
        norm = jnp.sum(WT[i], axis=0, keepdims=True)
        f = freq_of(i)
        part = jnp.where((rows8 == f) & live, quad, part)
        part = jnp.where((rows8 == f + 4) & live, norm, part)
    R1[0] = part

    ones = []
    for j in range(1, n_row):
        copy = remote(R1.at[0], R1.at[j], r1_send.at[j], r1_recv.at[j], ((r + j) % n_row, c, q))
        copy.start()
        ones.append(copy)

    def sent(ref, sem):
        remote(ref, ref, sem, b_recv.at[0, 0], sib).wait_send()

    whole = S.at[0]

    @pl.when((d != 4) & (d != 7) | ends)
    def _():
        sent(whole, up_send)

    @pl.when((d != 4) & (d != 1) | ends)
    def _():
        sent(whole, dn_send)

    @pl.when(~ends)
    def _():
        sent(whole, z_send)

    def sib_sent(i, carry):
        sent(whole, s_send.at[i])
        return carry

    lax.fori_loop(0, n_slots, sib_sent, 0)

    for copy in ones:
        copy.wait_recv()
    summed = R1[0]
    for j in range(1, n_row):
        summed += R1[j]
    share = slab // n_row
    mine = pltpu.roll(summed, (slab - share * r) % slab, 1)
    R2[0] = mine[:, 0:128]
    twos = []
    for j in range(1, n_col):
        copy = remote(R2.at[0], R2.at[j], r2_send.at[j], r2_recv.at[j], (r, (c + j) % n_col, q))
        copy.start()
        twos.append(copy)
    for copy in ones:
        copy.wait_send()
    for copy in twos:
        copy.wait_recv()
    totals = R2[0]
    for j in range(1, n_col):
        totals += R2[j]
    own = share // n_col
    totals = pltpu.roll(totals, (128 - own * c) % 128, 1)
    power = totals[0:4] / totals[4:8]
    pow_ref[...] = power[:, 0:own]
    R3[q] = jnp.broadcast_to(jnp.sum(power, axis=0, keepdims=True), (8, 128))
    threes = []
    for j in range(1, n_freq):
        copy = remote(R3.at[q], R3.at[q], r3_send.at[j], r3_recv.at[q], (r, c, (q + j) % n_freq))
        copy.start()
        threes.append(copy)
    for copy in twos:
        copy.wait_send()
    for j in range(1, n_freq):
        g = (q + j) % n_freq
        remote(R3.at[g], R3.at[g], r3_send.at[j], r3_recv.at[g], sib).wait_recv()
    surface = R3[0]
    for j in range(1, n_freq):
        surface += R3[j]
    surf_ref[...] = surface[0:1, 0:own] / total_freqs
    for copy in threes:
        copy.wait_send()


def solution(mesh):
    n_row, n_col, n_freq = (mesh.shape[a] for a in ("row", "col", "freq"))
    hbm = pl.BlockSpec(memory_space=pl.ANY)
    vmem = pl.BlockSpec(memory_space=pltpu.VMEM)

    def local(covariance, replica_table, slab_index):
        freqs, _, ch, table = replica_table.shape
        slab = slab_index.shape[0]
        own = slab // (n_row * n_col)
        sizes = (n_row, n_col, n_freq, ch, slab, table, freqs * n_freq)
        dma = pltpu.SemaphoreType.DMA
        power, surface = pl.pallas_call(
            functools.partial(kernel, sizes),
            out_shape=(jax.ShapeDtypeStruct((freqs, own), F32), jax.ShapeDtypeStruct((1, own), F32)),
            in_specs=[hbm, hbm, vmem],
            out_specs=(vmem, vmem),
            scratch_shapes=[
                pltpu.VMEM((freqs, 2, ch, table), BF16),
                pltpu.VMEM((freqs, 2 * ch, 2 * ch), BF16),
                pltpu.VMEM((freqs, 2 * ch, 2 * slab), BF16),
                pltpu.VMEM((table, slab), BF16),
                pltpu.VMEM((freqs, 2 * ch, 2 * slab), F32),
                pltpu.VMEM((3, ch, 2 * slab), BF16),
                pltpu.VMEM((freqs, ch, 2 * slab), BF16),
                pltpu.VMEM((freqs, 8, 2 * slab), F32),
                pltpu.VMEM((freqs, 8, slab), F32),
                pltpu.VMEM((n_row, 8, slab), F32),
                pltpu.VMEM((n_col, 8, 128), F32),
                pltpu.VMEM((n_freq, 8, 128), F32),
                dma((4,)), dma((4, 4)), dma((3, NCH)), dma((4, NCH)), dma, dma, dma, dma((4,)),
                dma((n_row,)), dma((n_row,)), dma((n_col,)), dma((n_col,)), dma((n_freq,)), dma((n_freq,)),
            ],
            compiler_params=pltpu.CompilerParams(
                collective_id=0, has_side_effects=True, vmem_limit_bytes=40 * 2**20),
        )(covariance, replica_table, slab_index.reshape(1, slab))
        return power, surface.reshape(own)

    in_specs = (P("freq", None, "row", "col"), P("freq", None, "col", None), P())
    out_specs = (P("freq", ("row", "col")), P(("row", "col")))
    return jax.shard_map(local, mesh=mesh, in_specs=in_specs, out_specs=out_specs, check_vma=False)
```

```python
import functools

import jax
import jax.numpy as jnp
from jax import lax
from jax.experimental import pallas as pl
from jax.experimental.pallas import tpu as pltpu
from jax.sharding import PartitionSpec as P

MESH = pl.DeviceIdType.MESH
F32 = jnp.float32
BF16 = jnp.bfloat16
NCH = 16
LAG = 6
SIB_LAG = 3


def kernel(sizes, cov, tbl, idx, pow_ref, surf_ref,
           T, C, X, OH, IM, B, S, ACC, WT, R1, R2, R3,
           tsem, csem, b_recv, s_recv, up_send, dn_send, z_send, s_send,
           r1_send, r1_recv, r2_send, r2_recv, r3_send, r3_recv):
    n_row, n_col, n_freq, ch, slab, table, total_freqs = sizes
    cr = ch // NCH
    r = lax.axis_index("row")
    c = lax.axis_index("col")
    q = lax.axis_index("freq")
    y = c // 2
    k = c % 2
    zl = r // 4
    d = (y - r + 8) % 8
    up = (r, (c + 2) % 16, q)
    down = (r, (c + 14) % 16, q)
    mate = ((r + 4) % 8, c, q)
    up_mate = ((r + 4) % 8, (c + 2) % 16, q)
    down_mate = ((r + 4) % 8, (c + 14) % 16, q)
    sib = (r, c + 1 - 2 * k, q)

    barrier = pltpu.get_barrier_semaphore()
    for j in range(1, n_col):
        pl.semaphore_signal(barrier, inc=1, device_id=(r, (c + j) % n_col, q), device_id_type=MESH)
    for j in range(1, n_row):
        pl.semaphore_signal(barrier, inc=1, device_id=((r + j) % n_row, c, q), device_id_type=MESH)
    for j in range(1, n_freq):
        pl.semaphore_signal(barrier, inc=1, device_id=(r, c, (q + j) % n_freq), device_id_type=MESH)

    for to in (up_mate, down_mate):
        pl.semaphore_signal(barrier, inc=1, device_id=to, device_id_type=MESH)

    ends = (d == 0) | (d == 4)
    base = jnp.where(d >= 5, 2, 0)
    n_slots = jnp.where(d == 0, 4, 2)

    def freq_of(i):
        first = jnp.where(i == 0, base + zl, jnp.where(ends, 2 + zl, base + 1 - zl))
        return jnp.where(i < 2, first, jnp.where(i == 2, 1 - zl, 3 - zl))

    def table_copy(i):
        return pltpu.make_async_copy(tbl.at[freq_of(i)], T.at[i], tsem.at[i])

    def cov_copies(i):
        out = []
        for part in range(2):
            for half in range(2):
                rows = pl.ds(pl.multiple_of((k if half == 0 else 1 - k) * ch, ch), ch)
                out.append(pltpu.make_async_copy(
                    cov.at[freq_of(i), part, rows, :],
                    C.at[i, pl.ds(half * ch, ch), pl.ds(part * ch, ch)],
                    csem.at[i, 2 * part + half]))
        return out

    def start_table(i, carry):
        table_copy(i).start()
        return carry

    def start_cov(i, carry):
        for copy in cov_copies(i):
            copy.start()
        return carry

    lax.fori_loop(0, n_slots, start_table, 0)
    lax.fori_loop(0, n_slots, start_cov, 0)

    points = lax.broadcasted_iota(jnp.int32, (table, slab), 0)
    OH[...] = jnp.where(points == idx[...], 1.0, 0.0).astype(BF16)
    ACC[...] = jnp.zeros_like(ACC)
    WT[...] = jnp.zeros_like(WT)

    def chunk(j):
        return pl.ds(pl.multiple_of(j * cr, cr), cr)

    def remote(src, dst, send, recv, to):
        return pltpu.make_async_remote_copy(
            src_ref=src, dst_ref=dst, send_sem=send, recv_sem=recv, device_id=to, device_id_type=MESH)

    to_up = jnp.where(d <= 3, 0, 2)
    to_down = jnp.where((d == 0) | (d >= 6), 0, jnp.where(d == 5, 1, 2))
    from_down = jnp.where(d <= 4, 0, 2)
    from_up = jnp.where(d >= 5, 0, jnp.where(d == 4, 1, 2))

    def send_up(src, j):
        return remote(src, B.at[to_up, chunk(j)], up_send, b_recv.at[to_up, j], up)

    def send_down(src, j):
        return remote(src, B.at[to_down, chunk(j)], dn_send, b_recv.at[to_down, j], down)

    def send_mate(src, j, to=mate):
        return remote(src, B.at[1, chunk(j)], z_send, b_recv.at[1, j], to)

    def send_sib(src, i, j):
        return remote(src, S.at[i, chunk(j)], s_send.at[i], s_recv.at[i, j], sib)

    def own_rows(i, j):
        return X.at[i, chunk(j), :]

    def gather(i, carry):
        table_copy(i).wait()
        both = jnp.dot(T[i].reshape(2 * ch, table), OH[...], preferred_element_type=F32)
        a, b = both[:ch], both[ch:]
        na, nb = a.astype(BF16), b.astype(BF16)
        X[i, 0:ch, 0:slab] = na
        X[i, 0:ch, slab:2 * slab] = nb
        X[i, ch:2 * ch, 0:slab] = -nb
        X[i, ch:2 * ch, slab:2 * slab] = na

        @pl.when(d == 0)
        def _():
            WT[i] = jnp.sum((a * a + b * b).reshape(ch // 8, 8, slab), axis=0)

        @pl.when(i == 0)
        def _():
            pl.semaphore_wait(barrier, n_col + n_row + n_freq - 1)

        @pl.when(ends & (i == 0))
        def _():
            def go(j, carry):
                send_up(own_rows(i, j), j).start()
                return carry
            lax.fori_loop(0, NCH, go, 0)

        @pl.when(ends & (i == 1))
        def _():
            def go(j, carry):
                send_down(own_rows(i, j), j).start()
                return carry
            lax.fori_loop(0, NCH, go, 0)

        @pl.when(d == 0)
        def _():
            def go(j, carry):
                send_sib(own_rows(i, j), i, j).start()
                return carry
            lax.fori_loop(0, NCH, go, 0)

        return carry

    lax.fori_loop(0, n_slots, gather, 0)

    def image(i, carry):
        for copy in cov_copies(i):
            copy.wait()
        IM[i] = jnp.dot(C[i], X[i], preferred_element_type=F32)
        return carry

    lax.fori_loop(0, n_slots, image, 0)

    def wait_in(slot, j):
        remote(B.at[slot, chunk(j)], B.at[slot, chunk(j)], z_send, b_recv.at[slot, j], sib).wait_recv()

    def wait_sib(i, j):
        remote(S.at[i, chunk(j)], S.at[i, chunk(j)], z_send, s_recv.at[i, j], sib).wait_recv()

    def fold(w, im):
        return jnp.sum((w.astype(F32) * im).reshape(cr // 8, 8, 2 * slab), axis=0)

    def combine(own, i, j):
        mine = fold(own[...], IM[i, chunk(j), :])
        other = pl.ds(pl.multiple_of(ch + j * cr, cr), cr)
        ACC[i] += mine + fold(S[i, chunk(j), :], IM[i, other, :])

    @pl.when(d == 0)
    def _():
        def each(m, carry):
            i, j = m // NCH, m % NCH
            wait_sib(i, j)
            combine(own_rows(i, j), i, j)
            return carry
        lax.fori_loop(0, 4 * NCH, each, 0)

    hops = jnp.where(d <= 4, d, 8 - d)

    @pl.when(d != 0)
    def _():
        lag_p = (jnp.where(d <= 4, d, d - 4) - 1) * LAG
        lag_m = (jnp.where(d >= 4, 8 - d, 4 - d) - 1) * LAG
        lag_z = jnp.where(hops == 3, 2 * LAG + 2, hops * LAG)
        lag_0 = (hops - 1) * LAG + SIB_LAG
        lag_1 = jnp.where(d == 4, 3 * LAG, lag_z) + SIB_LAG

        def within(j):
            return (j >= 0) & (j < NCH)

        def step(t, carry):
            jp = t - lag_p

            @pl.when(within(jp) & (d != 7))
            def _():
                wait_in(from_down, jp)
                here = B.at[from_down, chunk(jp)]

                @pl.when((d != 4) & (d != 6))
                def _():
                    send_up(here, jp).start()

                @pl.when(d <= 4)
                def _():
                    send_sib(here, 0, jp).start()

                @pl.when(d >= 5)
                def _():
                    send_mate(here, jp).start()

                @pl.when(d == 6)
                def _():
                    send_mate(here, jp, up_mate).start()

            jm = t - lag_m

            @pl.when(within(jm) & (d != 1))
            def _():
                wait_in(from_up, jm)
                here = B.at[from_up, chunk(jm)]

                @pl.when((d != 4) & (d != 2))
                def _():
                    send_down(here, jm).start()

                @pl.when(d >= 4)
                def _():
                    send_sib(here, from_up, jm).start()

                @pl.when(d <= 3)
                def _():
                    send_mate(here, jm).start()

                @pl.when(d == 2)
                def _():
                    send_mate(here, jm, down_mate).start()

            jz = t - lag_z

            @pl.when(within(jz) & (d != 4))
            def _():
                wait_in(1, jz)
                send_sib(B.at[1, chunk(jz)], 1, jz).start()

            j0 = t - lag_0

            @pl.when(within(j0))
            def _():
                wait_sib(0, j0)
                combine(B.at[0, chunk(j0)], 0, j0)

            j1 = t - lag_1

            @pl.when(within(j1))
            def _():
                wait_sib(1, j1)
                combine(B.at[1, chunk(j1)], 1, j1)

            return carry

        lax.fori_loop(0, NCH + lag_1, step, 0)

    scale = jnp.where(d == 0, 1.0, 2.0).astype(F32)
    rows8 = lax.broadcasted_iota(jnp.int32, (8, slab), 0)
    part = jnp.zeros((8, slab), F32)
    for i in range(4):
        live = i < n_slots
        sums = (ACC[i, :, 0:slab] + ACC[i, :, slab:2 * slab]) * scale
        quad = jnp.sum(sums, axis=0, keepdims=True)
        norm = jnp.sum(WT[i], axis=0, keepdims=True)
        f = freq_of(i)
        part = jnp.where((rows8 == f) & live, quad, part)
        part = jnp.where((rows8 == f + 4) & live, norm, part)
    R1[0] = part

    ones = []
    for j in range(1, n_row):
        copy = remote(R1.at[0], R1.at[j], r1_send.at[j], r1_recv.at[j], ((r + j) % n_row, c, q))
        copy.start()
        ones.append(copy)

    def sent(ref, sem):
        remote(ref, ref, sem, b_recv.at[0, 0], sib).wait_send()

    whole = S.at[0]

    @pl.when((d != 6) & (d != 7))
    def _():
        sent(whole, up_send)

    @pl.when((d != 2) & (d != 1))
    def _():
        sent(whole, dn_send)

    @pl.when((d == 2) | (d == 3) | (d == 5) | (d == 6))
    def _():
        sent(whole, z_send)

    @pl.when((d == 2) | (d == 6))
    def _():
        sent(whole, z_send)

    def sib_sent(i, carry):
        sent(whole, s_send.at[i])
        return carry

    lax.fori_loop(0, n_slots, sib_sent, 0)

    for copy in ones:
        copy.wait_recv()
    summed = R1[0]
    for j in range(1, n_row):
        summed += R1[j]
    share = slab // n_row
    mine = pltpu.roll(summed, (slab - share * r) % slab, 1)
    R2[0] = mine[:, 0:128]
    twos = []
    for j in range(1, n_col):
        copy = remote(R2.at[0], R2.at[j], r2_send.at[j], r2_recv.at[j], (r, (c + j) % n_col, q))
        copy.start()
        twos.append(copy)
    for copy in ones:
        copy.wait_send()
    for copy in twos:
        copy.wait_recv()
    totals = R2[0]
    for j in range(1, n_col):
        totals += R2[j]
    own = share // n_col
    totals = pltpu.roll(totals, (128 - own * c) % 128, 1)
    power = totals[0:4] / totals[4:8]
    pow_ref[...] = power[:, 0:own]
    R3[q] = jnp.broadcast_to(jnp.sum(power, axis=0, keepdims=True), (8, 128))
    threes = []
    for j in range(1, n_freq):
        copy = remote(R3.at[q], R3.at[q], r3_send.at[j], r3_recv.at[q], (r, c, (q + j) % n_freq))
        copy.start()
        threes.append(copy)
    for copy in twos:
        copy.wait_send()
    for j in range(1, n_freq):
        g = (q + j) % n_freq
        remote(R3.at[g], R3.at[g], r3_send.at[j], r3_recv.at[g], sib).wait_recv()
    surface = R3[0]
    for j in range(1, n_freq):
        surface += R3[j]
    surf_ref[...] = surface[0:1, 0:own] / total_freqs
    for copy in threes:
        copy.wait_send()


def solution(mesh):
    n_row, n_col, n_freq = (mesh.shape[a] for a in ("row", "col", "freq"))
    hbm = pl.BlockSpec(memory_space=pltpu.HBM)
    vmem = pl.BlockSpec(memory_space=pltpu.VMEM)

    def local(covariance, replica_table, slab_index):
        freqs, _, ch, table = replica_table.shape
        slab = slab_index.shape[0]
        own = slab // (n_row * n_col)
        sizes = (n_row, n_col, n_freq, ch, slab, table, freqs * n_freq)
        dma = pltpu.SemaphoreType.DMA
        power, surface = pl.pallas_call(
            functools.partial(kernel, sizes),
            out_shape=(jax.ShapeDtypeStruct((freqs, own), F32), jax.ShapeDtypeStruct((1, own), F32)),
            in_specs=[hbm, hbm, vmem],
            out_specs=(vmem, vmem),
            scratch_shapes=[
                pltpu.VMEM((freqs, 2, ch, table), BF16),
                pltpu.VMEM((freqs, 2 * ch, 2 * ch), BF16),
                pltpu.VMEM((freqs, 2 * ch, 2 * slab), BF16),
                pltpu.VMEM((table, slab), BF16),
                pltpu.VMEM((freqs, 2 * ch, 2 * slab), F32),
                pltpu.VMEM((3, ch, 2 * slab), BF16),
                pltpu.VMEM((freqs, ch, 2 * slab), BF16),
                pltpu.VMEM((freqs, 8, 2 * slab), F32),
                pltpu.VMEM((freqs, 8, slab), F32),
                pltpu.VMEM((n_row, 8, slab), F32),
                pltpu.VMEM((n_col, 8, 128), F32),
                pltpu.VMEM((n_freq, 8, 128), F32),
                dma((4,)), dma((4, 4)), dma((3, NCH)), dma((4, NCH)), dma, dma, dma, dma((4,)),
                dma((n_row,)), dma((n_row,)), dma((n_col,)), dma((n_col,)), dma((n_freq,)), dma((n_freq,)),
            ],
            compiler_params=pltpu.CompilerParams(
                collective_id=0, has_side_effects=True, vmem_limit_bytes=63 * 2**20),
        )(covariance, replica_table, slab_index.reshape(1, slab))
        return power, surface.reshape(own)

    in_specs = (P("freq", None, "row", "col"), P("freq", None, "col", None), P())
    out_specs = (P("freq", ("row", "col")), P(("row", "col")))
    return jax.shard_map(local, mesh=mesh, in_specs=in_specs, out_specs=out_specs, check_vma=False)
```

```python
import functools

import jax
import jax.numpy as jnp
from jax import lax
from jax.experimental import pallas as pl
from jax.experimental.pallas import tpu as pltpu
from jax.sharding import PartitionSpec as P

MESH = pl.DeviceIdType.MESH
F32 = jnp.float32
BF16 = jnp.bfloat16
NCH = 16
LAG = 6
SIB_LAG = 3
GREET = 6
ROUNDS = 5


def kernel(sizes, cov, tbl, idx, pow_ref, surf_ref,
           T, C, X, OH, IM, B, S, ACC, WT, A0, R0, A1, R1, A2, R2,
           tsem, csem, b_recv, s_recv, up_send, dn_send, z_send, s_send,
           a0_send, a0_recv, a1_send, a1_recv, a2_send, a2_recv, gossip):
    n_row, n_col, n_freq, ch, slab, table, total_freqs = sizes
    cr = ch // NCH
    r = lax.axis_index("row")
    c = lax.axis_index("col")
    q = lax.axis_index("freq")
    x = r % 4
    y = c // 2
    k = c % 2
    zl = r // 4
    z = 2 * q + zl
    d = (y - r + 8) % 8
    up = (r, (c + 2) % 16, q)
    down = (r, (c + 14) % 16, q)
    mate = ((r + 4) % 8, c, q)
    up_mate = ((r + 4) % 8, (c + 2) % 16, q)
    down_mate = ((r + 4) % 8, (c + 14) % 16, q)
    sib = (r, c + 1 - 2 * k, q)
    z_up, z_down = (z + 1) % 8, (z + 7) % 8
    near = [
        up, down, sib,
        (zl * 4 + (x + 1) % 4, c, q), (zl * 4 + (x + 3) % 4, c, q),
        ((z_up % 2) * 4 + x, c, z_up // 2), ((z_down % 2) * 4 + x, c, z_down // 2),
    ]

    barrier = pltpu.get_barrier_semaphore()
    greeted = near + [up_mate, down_mate]
    for to in greeted:
        pl.semaphore_signal(barrier, inc=1, device_id=to, device_id_type=MESH)

    ends = (d == 0) | (d == 4)
    base = jnp.where(d >= 5, 2, 0)
    n_slots = jnp.where(d == 0, 4, 2)

    def freq_of(i):
        first = jnp.where(i == 0, base + zl, jnp.where(ends, 2 + zl, base + 1 - zl))
        low, high = jnp.where(ends, 1 - zl, 2 - base + zl), jnp.where(ends, 3 - zl, 3 - base - zl)
        return jnp.where(i < 2, first, jnp.where(i == 2, low, high))

    def table_copy(i):
        return pltpu.make_async_copy(tbl.at[freq_of(i)], T.at[i], tsem.at[i])

    def cov_copies(i):
        out = []
        for part in range(2):
            for half in range(2):
                rows = pl.ds(pl.multiple_of((k if half == 0 else 1 - k) * ch, ch), ch)
                out.append(pltpu.make_async_copy(
                    cov.at[freq_of(i), part, rows, :],
                    C.at[i, pl.ds(half * ch, ch), pl.ds(part * ch, ch)],
                    csem.at[i, 2 * part + half]))
        return out

    def start_table(i, carry):
        table_copy(i).start()
        return carry

    def start_cov(i, carry):
        for copy in cov_copies(i):
            copy.start()
        return carry

    lax.fori_loop(0, 4, start_table, 0)
    lax.fori_loop(0, n_slots, start_cov, 0)

    share = slab // n_row
    own = share // n_col
    points = lax.broadcasted_iota(jnp.int32, (table, slab), 0)
    taken = jnp.where(points == idx[...], 1.0, 0.0).astype(BF16)
    lane = lax.broadcasted_iota(jnp.int32, (slab, slab), 1)
    source = lane % n_row * share + lane % 128 // n_row * own + lane // 128
    order = jnp.where(lax.broadcasted_iota(jnp.int32, (slab, slab), 0) == source, 1.0, 0.0).astype(BF16)
    OH[...] = jnp.dot(taken, order, preferred_element_type=F32).astype(BF16)
    ACC[...] = jnp.zeros_like(ACC)
    A0[...] = jnp.zeros_like(A0)
    A1[...] = jnp.zeros_like(A1)

    def chunk(j):
        return pl.ds(pl.multiple_of(j * cr, cr), cr)

    def remote(src, dst, send, recv, to):
        return pltpu.make_async_remote_copy(
            src_ref=src, dst_ref=dst, send_sem=send, recv_sem=recv, device_id=to, device_id_type=MESH)

    to_up = jnp.where(d <= 3, 0, 2)
    to_down = jnp.where((d == 0) | (d >= 6), 0, jnp.where(d == 5, 1, 2))
    from_down = jnp.where(d <= 4, 0, 2)
    from_up = jnp.where(d >= 5, 0, jnp.where(d == 4, 1, 2))

    def send_up(src, j):
        return remote(src, B.at[to_up, chunk(j)], up_send, b_recv.at[to_up, j], up)

    def send_down(src, j):
        return remote(src, B.at[to_down, chunk(j)], dn_send, b_recv.at[to_down, j], down)

    def send_mate(src, j, to=mate):
        return remote(src, B.at[1, chunk(j)], z_send, b_recv.at[1, j], to)

    def send_sib(src, i, j):
        return remote(src, S.at[i, chunk(j)], s_send.at[i], s_recv.at[i, j], sib)

    def own_rows(i, j):
        return X.at[i, chunk(j), :]

    def gather(i, carry):
        table_copy(i).wait()
        both = jnp.dot(T[i].reshape(2 * ch, table), OH[...], preferred_element_type=F32)
        a, b = both[:ch], both[ch:]
        na, nb = a.astype(BF16), b.astype(BF16)
        X[i, 0:ch, 0:slab] = na
        X[i, 0:ch, slab:2 * slab] = nb
        X[i, ch:2 * ch, 0:slab] = -nb
        X[i, ch:2 * ch, slab:2 * slab] = na

        WT[i] = jnp.sum((a * a + b * b).reshape(ch // 8, 8, slab), axis=0)

        @pl.when(i == 0)
        def _():
            pl.semaphore_wait(barrier, len(greeted))

        @pl.when(ends & (i == 0))
        def _():
            def go(j, carry):
                send_up(own_rows(i, j), j).start()
                return carry
            lax.fori_loop(0, NCH, go, 0)

        @pl.when(ends & (i == 1))
        def _():
            def go(j, carry):
                send_down(own_rows(i, j), j).start()
                return carry
            lax.fori_loop(0, NCH, go, 0)

        @pl.when(d == 0)
        def _():
            def go(j, carry):
                send_sib(own_rows(i, j), i, j).start()
                return carry
            lax.fori_loop(0, NCH, go, 0)

        return carry

    lax.fori_loop(0, 4, gather, 0)

    def image(i, carry):
        for copy in cov_copies(i):
            copy.wait()
        IM[i] = jnp.dot(C[i], X[i], preferred_element_type=F32)
        return carry

    lax.fori_loop(0, n_slots, image, 0)

    def wait_in(slot, j):
        remote(B.at[slot, chunk(j)], B.at[slot, chunk(j)], z_send, b_recv.at[slot, j], sib).wait_recv()

    def wait_sib(i, j):
        remote(S.at[i, chunk(j)], S.at[i, chunk(j)], z_send, s_recv.at[i, j], sib).wait_recv()

    def fold(w, im):
        return jnp.sum((w.astype(F32) * im).reshape(cr // 8, 8, 2 * slab), axis=0)

    def combine(own, i, j):
        mine = fold(own[...], IM[i, chunk(j), :])
        other = pl.ds(pl.multiple_of(ch + j * cr, cr), cr)
        ACC[i] += mine + fold(S[i, chunk(j), :], IM[i, other, :])

    def tiles(to, sums):
        lines = lax.broadcasted_iota(jnp.int32, (16, 128), 0)
        part = jnp.zeros((16, 128), F32)
        for i in range(4):
            total = jnp.sum(sums(i), axis=0, keepdims=True)
            for m in range(own):
                part = jnp.where(lines == own * freq_of(i) + m, total[:, 128 * m:128 * (m + 1)], part)
        to[:, :, 0:16] = part.T.reshape(n_col, n_row, 16)

    def to_column(src, dst, send, recv):
        def go(j, carry):
            to = (c + j) % n_col
            remote(src.at[to], dst.at[j], send, recv, (r, to, q)).start()
            return carry
        lax.fori_loop(1, n_col, go, 0)

    def column_wait(dst, send, recv):
        others = dst.at[pl.ds(1, n_col - 1)]
        return remote(others, others, send, recv, sib)

    def greet(n):
        for to in near:
            pl.semaphore_signal(gossip.at[n], inc=1, device_id=to, device_id_type=MESH)

    tiles(A0, lambda i: WT[i])

    hops = jnp.where(d <= 4, d, 8 - d)

    lag_p = (jnp.where(d <= 4, d, d - 4) - 1) * LAG
    lag_m = (jnp.where(d >= 4, 8 - d, 4 - d) - 1) * LAG
    lag_z = jnp.where(hops == 3, 2 * LAG + 2, hops * LAG)
    lag_0 = (hops - 1) * LAG + SIB_LAG
    lag_1 = jnp.where(d == 4, 3 * LAG, lag_z) + SIB_LAG
    off = d != 0

    def within(j):
        return (j >= 0) & (j < NCH)

    def step(t, carry):
        jp = t - lag_p

        @pl.when(off & within(jp) & (d != 7))
        def _():
            wait_in(from_down, jp)
            here = B.at[from_down, chunk(jp)]

            @pl.when((d != 4) & (d != 6))
            def _():
                send_up(here, jp).start()

            @pl.when(d <= 4)
            def _():
                send_sib(here, 0, jp).start()

            @pl.when(d >= 5)
            def _():
                send_mate(here, jp).start()

            @pl.when(d == 6)
            def _():
                send_mate(here, jp, up_mate).start()

        jm = t - lag_m

        @pl.when(off & within(jm) & (d != 1))
        def _():
            wait_in(from_up, jm)
            here = B.at[from_up, chunk(jm)]

            @pl.when((d != 4) & (d != 2))
            def _():
                send_down(here, jm).start()

            @pl.when(d >= 4)
            def _():
                send_sib(here, from_up, jm).start()

            @pl.when(d <= 3)
            def _():
                send_mate(here, jm).start()

            @pl.when(d == 2)
            def _():
                send_mate(here, jm, down_mate).start()

        jz = t - lag_z

        @pl.when(off & within(jz) & (d != 4))
        def _():
            wait_in(1, jz)
            send_sib(B.at[1, chunk(jz)], 1, jz).start()

        j0 = t - lag_0

        @pl.when(off & within(j0))
        def _():
            wait_sib(0, j0)
            combine(B.at[0, chunk(j0)], 0, j0)

        j1 = t - lag_1

        @pl.when(off & within(j1))
        def _():
            wait_sib(1, j1)
            combine(B.at[1, chunk(j1)], 1, j1)

        js = t - GREET

        @pl.when((d == 0) & within(js))
        def _():
            for i in range(4):
                wait_sib(i, js)
                combine(own_rows(i, js), i, js)

        @pl.when((t % GREET == 0) & (t <= ROUNDS * GREET))
        def _():
            n = t // GREET

            @pl.when(n > 0)
            def _():
                pl.semaphore_wait(gossip.at[n - 1], len(near))

            @pl.when(n < ROUNDS)
            def _():
                greet(n)

            @pl.when(n == ROUNDS - 1)
            def _():
                to_column(A0, R0, a0_send, a0_recv)

        return carry

    lax.fori_loop(0, NCH + 3 * LAG + SIB_LAG + 1, step, 0)

    scale = jnp.where(d == 0, 1.0, 2.0).astype(F32)
    tiles(A1, lambda i: (ACC[i, :, 0:slab] + ACC[i, :, slab:2 * slab]) * scale)
    to_column(A1, R1, a1_send, a1_recv)
    column_wait(R0, a0_send, a0_recv).wait()
    norm = A0[c]
    for j in range(1, n_col):
        norm += R0[j]
    lanes = lax.broadcasted_iota(jnp.int32, (8, 128), 1)
    used = lanes < 4 * own
    norm = jnp.where(used, norm, 1.0)

    def sent(ref, sem):
        remote(ref, ref, sem, b_recv.at[0, 0], sib).wait_send()

    whole = S.at[0]

    @pl.when((d != 6) & (d != 7))
    def _():
        sent(whole, up_send)

    @pl.when((d != 2) & (d != 1))
    def _():
        sent(whole, dn_send)

    @pl.when((d == 2) | (d == 3) | (d == 5) | (d == 6))
    def _():
        sent(whole, z_send)

    @pl.when((d == 2) | (d == 6))
    def _():
        sent(whole, z_send)

    def sib_sent(i, carry):
        sent(whole, s_send.at[i])
        return carry

    lax.fori_loop(0, n_slots, sib_sent, 0)

    column_wait(R1, a1_send, a1_recv).wait()
    form = A1[c]
    for j in range(1, n_col):
        form += R1[j]
    power = jnp.where(used, form / norm, 0.0)
    total = power
    for f in range(1, 4):
        total += pltpu.roll(power, 128 - own * f, 1)
    both = jnp.where(used, power, pltpu.roll(total, 64, 1))
    for j in range(n_row):
        A2[j] = both[j:j + 1]
    me = q * n_row + r
    R2[me] = A2[r]

    def go(j, carry):
        to, at = (r + j) % n_row, (q + j // n_row) % n_freq
        remote(A2.at[to], R2.at[me], a2_send, a2_recv, (to, c, at)).start()
        return carry

    lax.fori_loop(1, n_row * n_freq, go, 0)
    others = R2.at[pl.ds(1, n_row * n_freq - 1)]
    remote(others, others, a2_send, a2_recv, sib).wait()
    whole_power = R2[q * n_row]
    for j in range(1, n_row):
        whole_power += R2[q * n_row + j]
    surface = R2[0]
    for j in range(1, n_row * n_freq):
        surface += R2[j]
    line = lax.broadcasted_iota(jnp.int32, (4, 128), 0)
    out = jnp.broadcast_to(whole_power, (4, 128))
    for f in range(1, 4):
        out = jnp.where(line == f, pltpu.roll(whole_power, 128 - own * f, 1), out)
    pow_ref[...] = out[:, 0:own]
    surf_ref[...] = pltpu.roll(surface, 64, 1)[:, 0:own] / total_freqs


def solution(mesh):
    n_row, n_col, n_freq = (mesh.shape[a] for a in ("row", "col", "freq"))
    hbm = pl.BlockSpec(memory_space=pltpu.HBM)
    vmem = pl.BlockSpec(memory_space=pltpu.VMEM)

    def local(covariance, replica_table, slab_index):
        freqs, _, ch, table = replica_table.shape
        slab = slab_index.shape[0]
        own = slab // (n_row * n_col)
        sizes = (n_row, n_col, n_freq, ch, slab, table, freqs * n_freq)
        dma = pltpu.SemaphoreType.DMA
        power, surface = pl.pallas_call(
            functools.partial(kernel, sizes),
            out_shape=(jax.ShapeDtypeStruct((freqs, own), F32), jax.ShapeDtypeStruct((1, own), F32)),
            in_specs=[hbm, hbm, vmem],
            out_specs=(vmem, vmem),
            scratch_shapes=[
                pltpu.VMEM((freqs, 2, ch, table), BF16),
                pltpu.VMEM((freqs, 2 * ch, 2 * ch), BF16),
                pltpu.VMEM((freqs, 2 * ch, 2 * slab), BF16),
                pltpu.VMEM((table, slab), BF16),
                pltpu.VMEM((freqs, 2 * ch, 2 * slab), F32),
                pltpu.VMEM((3, ch, 2 * slab), BF16),
                pltpu.VMEM((freqs, ch, 2 * slab), BF16),
                pltpu.VMEM((freqs, 8, 2 * slab), F32),
                pltpu.VMEM((freqs, 8, slab), F32),
                pltpu.VMEM((n_col, n_row, 128), F32),
                pltpu.VMEM((n_col, n_row, 128), F32),
                pltpu.VMEM((n_col, n_row, 128), F32),
                pltpu.VMEM((n_col, n_row, 128), F32),
                pltpu.VMEM((n_row, 1, 128), F32),
                pltpu.VMEM((n_row * n_freq, 1, 128), F32),
                dma((4,)), dma((4, 4)), dma((3, NCH)), dma((4, NCH)), dma, dma, dma, dma((4,)),
                dma, dma, dma, dma, dma, dma, pltpu.SemaphoreType.REGULAR((ROUNDS,)),
            ],
            compiler_params=pltpu.CompilerParams(
                collective_id=0, has_side_effects=True, vmem_limit_bytes=63 * 2**20),
        )(covariance, replica_table, slab_index.reshape(1, slab))
        return power, surface.reshape(own)

    in_specs = (P("freq", None, "row", "col"), P("freq", None, "col", None), P())
    out_specs = (P("freq", ("row", "col")), P(("row", "col")))
    return jax.shard_map(local, mesh=mesh, in_specs=in_specs, out_specs=out_specs, check_vma=False)
```

```python
import functools

import jax
import jax.numpy as jnp
from jax import lax
from jax.experimental import pallas as pl
from jax.experimental.pallas import tpu as pltpu
from jax.sharding import PartitionSpec as P

MESH = pl.DeviceIdType.MESH
F32 = jnp.float32
BF16 = jnp.bfloat16
NCH = 16
LAG = 6
MIN_LAG = 8
GREET = 10
ROUNDS = 3


def kernel(sizes, cov, tbl, idx, pow_ref, surf_ref,
           T, C, X, OH, IM, SI, B, ACC, WT, A0, R0, A1, R1, A2, R2,
           tsem, csem, b_recv, s_recv, up_send, dn_send, z_send, s_send,
           a0_send, a0_recv, a1_send, a1_recv, a2_send, a2_recv, gossip):
    n_row, n_col, n_freq, ch, slab, table, total_freqs = sizes
    cr = ch // NCH
    r = lax.axis_index("row")
    c = lax.axis_index("col")
    q = lax.axis_index("freq")
    y = c // 2
    k = c % 2
    zl = r // 4
    d = (y - r + 8) % 8
    up = (r, (c + 2) % 16, q)
    down = (r, (c + 14) % 16, q)
    mate = ((r + 4) % 8, c, q)
    up_mate = ((r + 4) % 8, (c + 2) % 16, q)
    down_mate = ((r + 4) % 8, (c + 14) % 16, q)
    sib = (r, c + 1 - 2 * k, q)
    across = ((r + 4) % 8, c, (q + jnp.where(zl == 1, 1, n_freq - 1)) % n_freq)
    column = [(r, (c + j) % n_col, q) for j in range(1, n_col)]
    rows = [((r + j) % n_row, c, q) for j in range(1, n_row)]
    near = rows + [across]

    barrier = pltpu.get_barrier_semaphore()
    greeted = column + near + [up_mate, down_mate]
    for to in greeted:
        pl.semaphore_signal(barrier, inc=1, device_id=to, device_id_type=MESH)

    ends = (d == 0) | (d == 4)
    base = jnp.where(d >= 5, 2, 0)
    n_slots = jnp.where(d == 0, 4, 2)

    def freq_of(i):
        first = jnp.where(i == 0, base + zl, jnp.where(ends, 2 + zl, base + 1 - zl))
        low, high = jnp.where(ends, 1 - zl, 2 - base + zl), jnp.where(ends, 3 - zl, 3 - base - zl)
        return jnp.where(i < 2, first, jnp.where(i == 2, low, high))

    def table_copy(i):
        return pltpu.make_async_copy(tbl.at[freq_of(i)], T.at[i], tsem.at[i])

    def cov_copies(i):
        out = []
        for part in range(2):
            for half in range(2):
                rows = pl.ds(pl.multiple_of((k if half == 0 else 1 - k) * ch, ch), ch)
                out.append(pltpu.make_async_copy(
                    cov.at[freq_of(i), part, rows, :],
                    C.at[i, pl.ds(half * ch, ch), pl.ds(part * ch, ch)],
                    csem.at[i, 2 * part + half]))
        return out

    def start_table(i, carry):
        table_copy(i).start()
        return carry

    def start_cov(i, carry):
        for copy in cov_copies(i):
            copy.start()
        return carry

    lax.fori_loop(0, 4, start_table, 0)
    lax.fori_loop(0, n_slots, start_cov, 0)

    share = slab // n_row
    own = share // n_col
    points = lax.broadcasted_iota(jnp.int32, (table, slab), 0)
    taken = jnp.where(points == idx[...].reshape(1, slab), 1.0, 0.0).astype(BF16)
    lane = lax.broadcasted_iota(jnp.int32, (slab, slab), 1)
    source = lane % n_row * share + lane % 128 // n_row * own + lane // 128
    order = jnp.where(lax.broadcasted_iota(jnp.int32, (slab, slab), 0) == source, 1.0, 0.0).astype(BF16)
    OH[...] = jnp.dot(taken, order, preferred_element_type=F32).astype(BF16)
    ACC[...] = jnp.zeros_like(ACC)

    def chunk(j):
        return pl.ds(pl.multiple_of(j * cr, cr), cr)

    def remote(src, dst, send, recv, to):
        return pltpu.make_async_remote_copy(
            src_ref=src, dst_ref=dst, send_sem=send, recv_sem=recv, device_id=to, device_id_type=MESH)

    to_up = jnp.where(d <= 3, 0, 2)
    to_down = jnp.where((d == 0) | (d >= 6), 0, jnp.where(d == 5, 1, 2))
    from_down = jnp.where(d <= 4, 0, 2)
    from_up = jnp.where(d >= 5, 0, jnp.where(d == 4, 1, 2))

    def send_up(src, j):
        return remote(src, B.at[to_up, chunk(j)], up_send, b_recv.at[to_up, j], up)

    def send_down(src, j):
        return remote(src, B.at[to_down, chunk(j)], dn_send, b_recv.at[to_down, j], down)

    def send_mate(src, j, to=mate):
        return remote(src, B.at[1, chunk(j)], z_send, b_recv.at[1, j], to)

    def send_image(i):
        return remote(IM.at[i, pl.ds(ch, ch)], SI.at[i], s_send.at[i], s_recv.at[i], sib)

    def own_rows(i, j):
        return X.at[i, chunk(j), :]

    def gather(i, carry):
        table_copy(i).wait()
        both = jnp.dot(T[i].reshape(2 * ch, table), OH[...], preferred_element_type=F32)
        a, b = both[:ch], both[ch:]
        na, nb = a.astype(BF16), b.astype(BF16)
        X[i, 0:ch, 0:slab] = na
        X[i, 0:ch, slab:2 * slab] = nb
        X[i, ch:2 * ch, 0:slab] = -nb
        X[i, ch:2 * ch, slab:2 * slab] = na

        WT[i] = jnp.sum((a * a + b * b).reshape(ch // 8, 8, slab), axis=0)

        @pl.when(i == 0)
        def _():
            pl.semaphore_wait(barrier, len(greeted))

        @pl.when(ends & (i == 0))
        def _():
            def go(j, carry):
                send_up(own_rows(i, j), j).start()
                return carry
            lax.fori_loop(0, NCH, go, 0)

        @pl.when(ends & (i == 1))
        def _():
            def go(j, carry):
                send_down(own_rows(i, j), j).start()
                return carry
            lax.fori_loop(0, NCH, go, 0)

        return carry

    lax.fori_loop(0, 4, gather, 0)

    def image(i, carry):
        for copy in cov_copies(i):
            copy.wait()
        IM[i] = jnp.dot(C[i], X[i], preferred_element_type=F32)
        send_image(i).start()
        return carry

    def wait_in(slot, j):
        remote(B.at[slot, chunk(j)], B.at[slot, chunk(j)], z_send, b_recv.at[slot, j], sib).wait_recv()

    def fold(w, im):
        return jnp.sum((w.astype(F32) * im).reshape(cr // 8, 8, 2 * slab), axis=0)

    def combine(replicas, i, j):
        @pl.when(j == 0)
        def _():
            send_image(i).wait_recv()

        total = IM[i, chunk(j), :] + SI[i, chunk(j), :]
        ACC[i] += fold(replicas[...], total)

    def lines(to, sums):
        line = lax.broadcasted_iota(jnp.int32, (n_col, 128), 0)
        group = lax.broadcasted_iota(jnp.int32, (n_col, 128), 1) // n_row
        out = jnp.zeros((n_col, 128), F32)
        for i in range(4):
            total = jnp.sum(sums(i), axis=0, keepdims=True)
            for m in range(own):
                kept = jnp.where(line == group, total[:, 128 * m:128 * (m + 1)], 0.0)
                for shift in (8, 16, 32, 64):
                    kept += pltpu.roll(kept, shift, 1)
                out = jnp.where(group == own * freq_of(i) + m, kept, out)
        for j in range(n_col):
            to[j] = out[j:j + 1]

    def to_column(src, dst, send, recv):
        def go(j, carry):
            to = (c + j) % n_col
            remote(src.at[to], dst.at[j], send, recv, (r, to, q)).start()
            return carry
        lax.fori_loop(1, n_col, go, 0)

    def column_wait(dst, send, recv):
        others = dst.at[pl.ds(1, n_col - 1)]
        return remote(others, others, send, recv, sib)

    def greet(n):
        for to in near:
            pl.semaphore_signal(gossip.at[n], inc=1, device_id=to, device_id_type=MESH)

    lax.fori_loop(0, n_slots, image, 0)
    lines(A0, lambda i: WT[i])
    to_column(A0, R0, a0_send, a0_recv)
    greet(0)

    hops = jnp.where(d <= 4, d, 8 - d)

    lag_p = (jnp.where(d <= 4, d, d - 4) - 1) * LAG
    lag_m = (jnp.where(d >= 4, 8 - d, 4 - d) - 1) * LAG
    lag_z = jnp.where(hops == 3, 2 * LAG + 2, hops * LAG)
    lag_0 = jnp.maximum((hops - 1) * LAG, MIN_LAG)
    lag_1 = jnp.maximum(jnp.where(d == 4, 3 * LAG, lag_z), MIN_LAG)
    off = d != 0

    def within(j):
        return (j >= 0) & (j < NCH)

    def step(t, carry):
        jp = t - lag_p

        @pl.when(off & within(jp) & (d != 7))
        def _():
            wait_in(from_down, jp)
            here = B.at[from_down, chunk(jp)]

            @pl.when((d != 4) & (d != 6))
            def _():
                send_up(here, jp).start()

            @pl.when(d >= 5)
            def _():
                send_mate(here, jp).start()

            @pl.when(d == 6)
            def _():
                send_mate(here, jp, up_mate).start()

        jm = t - lag_m

        @pl.when(off & within(jm) & (d != 1))
        def _():
            wait_in(from_up, jm)
            here = B.at[from_up, chunk(jm)]

            @pl.when((d != 4) & (d != 2))
            def _():
                send_down(here, jm).start()

            @pl.when(d <= 3)
            def _():
                send_mate(here, jm).start()

            @pl.when(d == 2)
            def _():
                send_mate(here, jm, down_mate).start()

        jz = t - lag_z

        @pl.when(off & within(jz) & (d != 4))
        def _():
            wait_in(1, jz)

        j0 = t - lag_0

        @pl.when(off & within(j0))
        def _():
            combine(B.at[0, chunk(j0)], 0, j0)

        j1 = t - lag_1

        @pl.when(off & within(j1))
        def _():
            combine(B.at[1, chunk(j1)], 1, j1)

        js = t - MIN_LAG

        @pl.when((d == 0) & within(js))
        def _():
            def each(i, carry):
                combine(own_rows(i, js), i, js)
                return carry
            lax.fori_loop(0, 4, each, 0)

        for n in range(1, ROUNDS):
            @pl.when(t == n * GREET)
            def _():
                pl.semaphore_wait(gossip.at[n - 1], len(near))
                greet(n)

        return carry

    steps = jnp.where(d == 0, MIN_LAG, jnp.maximum(lag_0, lag_1))
    lax.fori_loop(0, NCH + jnp.maximum(steps, (ROUNDS - 1) * GREET + 1 - NCH), step, 0)

    scale = jnp.where(d == 0, 1.0, 2.0).astype(F32)
    lines(A1, lambda i: (ACC[i, :, 0:slab] + ACC[i, :, slab:2 * slab]) * scale)
    to_column(A1, R1, a1_send, a1_recv)
    column_wait(R0, a0_send, a0_recv).wait()
    norm = A0[c]
    for j in range(1, n_col):
        norm += R0[j]
    used = lax.broadcasted_iota(jnp.int32, (1, 128), 1) < 4 * own * n_row
    norm = jnp.where(used, norm, 1.0)

    def sent(ref, sem):
        remote(ref, ref, sem, b_recv.at[0, 0], sib).wait_send()

    whole = B.at[0]

    @pl.when((d != 6) & (d != 7))
    def _():
        sent(whole, up_send)

    @pl.when((d != 2) & (d != 1))
    def _():
        sent(whole, dn_send)

    @pl.when((d == 2) | (d == 3) | (d == 5) | (d == 6))
    def _():
        sent(whole, z_send)

    @pl.when((d == 2) | (d == 6))
    def _():
        sent(whole, z_send)

    def sib_sent(i, carry):
        send_image(i).wait_send()
        return carry

    lax.fori_loop(0, n_slots, sib_sent, 0)

    column_wait(R1, a1_send, a1_recv).wait()
    form = A1[c]
    for j in range(1, n_col):
        form += R1[j]
    power = jnp.where(used, form / norm, 0.0)
    stride = own * n_row
    total = power
    for f in range(1, 4):
        total += pltpu.roll(power, 128 - stride * f, 1)
    A2[...] = jnp.where(used, power, pltpu.roll(total, 4 * stride, 1))
    me = q * n_row + r
    R2[me] = A2[...]
    pl.semaphore_wait(gossip.at[ROUNDS - 1], len(near))

    def go(j, carry):
        to, at = (r + j) % n_row, (q + j // n_row) % n_freq
        remote(A2, R2.at[me], a2_send, a2_recv, (to, c, at)).start()
        return carry

    lax.fori_loop(1, n_row * n_freq, go, 0)
    others = R2.at[pl.ds(1, n_row * n_freq - 1)]
    remote(others, others, a2_send, a2_recv, sib).wait()
    power = R2[q * n_row]
    for j in range(1, n_row):
        power += R2[q * n_row + j]
    surface = R2[0]
    for j in range(1, n_row * n_freq):
        surface += R2[j]
    mine = (128 - r) % 128
    power = pltpu.roll(jnp.broadcast_to(power, (8, 128)), mine, 1)
    surface = pltpu.roll(jnp.broadcast_to(surface, (8, 128)), mine, 1)
    line = lax.broadcasted_iota(jnp.int32, (8, 128), 0)
    lane = lax.broadcasted_iota(jnp.int32, (8, 128), 1)
    out = power
    for f in range(4):
        for m in range(own):
            at = (own * f + m) * n_row - m
            out = jnp.where((line == f) & (lane == m), pltpu.roll(power, (128 - at) % 128, 1), out)
    total = surface
    for m in range(own):
        total = jnp.where(lane == m, pltpu.roll(surface, 128 - 4 * stride - m * n_row + m, 1), total)
    pow_ref[...] = out[0:4, 0:own]
    surf_ref[...] = total[0:1, 0:own] / total_freqs


def solution(mesh):
    n_row, n_col, n_freq = (mesh.shape[a] for a in ("row", "col", "freq"))
    hbm = pl.BlockSpec(memory_space=pltpu.HBM)
    vmem = pl.BlockSpec(memory_space=pltpu.VMEM)

    def local(covariance, replica_table, slab_index):
        freqs, _, ch, table = replica_table.shape
        slab = slab_index.shape[0]
        own = slab // (n_row * n_col)
        sizes = (n_row, n_col, n_freq, ch, slab, table, freqs * n_freq)
        dma = pltpu.SemaphoreType.DMA
        power, surface = pl.pallas_call(
            functools.partial(kernel, sizes),
            out_shape=(jax.ShapeDtypeStruct((freqs, own), F32), jax.ShapeDtypeStruct((1, own), F32)),
            in_specs=[hbm, hbm, vmem],
            out_specs=(vmem, vmem),
            scratch_shapes=[
                pltpu.VMEM((freqs, 2, ch, table), BF16),
                pltpu.VMEM((freqs, 2 * ch, 2 * ch), BF16),
                pltpu.VMEM((freqs, 2 * ch, 2 * slab), BF16),
                pltpu.VMEM((table, slab), BF16),
                pltpu.VMEM((freqs, 2 * ch, 2 * slab), F32),
                pltpu.VMEM((freqs, ch, 2 * slab), F32),
                pltpu.VMEM((3, ch, 2 * slab), BF16),
                pltpu.VMEM((freqs, 8, 2 * slab), F32),
                pltpu.VMEM((freqs, 8, slab), F32),
                pltpu.VMEM((n_col, 1, 128), F32),
                pltpu.VMEM((n_col, 1, 128), F32),
                pltpu.VMEM((n_col, 1, 128), F32),
                pltpu.VMEM((n_col, 1, 128), F32),
                pltpu.VMEM((1, 128), F32),
                pltpu.VMEM((n_row * n_freq, 1, 128), F32),
                dma((4,)), dma((4, 4)), dma((3, NCH)), dma((4,)), dma, dma, dma, dma((4,)),
                dma, dma, dma, dma, dma, dma, pltpu.SemaphoreType.REGULAR((ROUNDS,)),
            ],
            compiler_params=pltpu.CompilerParams(
                collective_id=0, has_side_effects=True, vmem_limit_bytes=63 * 2**20),
        )(covariance, replica_table, slab_index)
        return power, surface.reshape(own)

    in_specs = (P("freq", None, "row", "col"), P("freq", None, "col", None), P())
    out_specs = (P("freq", ("row", "col")), P(("row", "col")))
    return jax.shard_map(local, mesh=mesh, in_specs=in_specs, out_specs=out_specs, check_vma=False)
```

```python
import functools

import jax
import jax.numpy as jnp
from jax import lax
from jax.experimental import pallas as pl
from jax.experimental.pallas import tpu as pltpu
from jax.sharding import PartitionSpec as P

MESH = pl.DeviceIdType.MESH
F32 = jnp.float32
BF16 = jnp.bfloat16
NCH = 16
LAG = 6
MIN_LAG = 8
GREET = 10
ROUNDS = 3


def mod(a, n):
    return lax.rem(a, n)


def kernel(sizes, cov, tbl, idx, pow_ref, surf_ref,
           T, C, X, OH, IM, SI, B, ACC, WT, A0, R0, A1, R1, A2, R2,
           tsem, csem, b_recv, s_recv, up_send, dn_send, z_send, s_send,
           a0_send, a0_recv, a1_send, a1_recv, a2_send, a2_recv, gossip):
    n_row, n_col, n_freq, ch, slab, table, total_freqs = sizes
    cr = ch // NCH
    r = lax.axis_index("row")
    c = lax.axis_index("col")
    q = lax.axis_index("freq")
    y = lax.div(c, 2)
    k = mod(c, 2)
    zl = lax.div(r, 4)
    d = mod(y - r + 8, 8)
    up = (r, mod(c + 2, 16), q)
    down = (r, mod(c + 14, 16), q)
    mate = (mod(r + 4, 8), c, q)
    up_mate = (mod(r + 4, 8), mod(c + 2, 16), q)
    down_mate = (mod(r + 4, 8), mod(c + 14, 16), q)
    sib = (r, c + 1 - 2 * k, q)
    across = (mod(r + 4, 8), c, mod(q + jnp.where(zl == 1, 1, n_freq - 1), n_freq))
    column = [(r, mod(c + j, n_col), q) for j in range(1, n_col)]
    rows = [(mod(r + j, n_row), c, q) for j in range(1, n_row)]
    near = rows + [across]

    barrier = pltpu.get_barrier_semaphore()
    greeted = column + near + [up_mate, down_mate]
    for to in greeted:
        pl.semaphore_signal(barrier, inc=1, device_id=to, device_id_type=MESH)

    ends = (d == 0) | (d == 4)
    base = jnp.where(d >= 5, 2, 0)
    n_slots = jnp.where(d == 0, 4, 2)

    def freq_of(i):
        first = jnp.where(i == 0, base + zl, jnp.where(ends, 2 + zl, base + 1 - zl))
        low, high = jnp.where(ends, 1 - zl, 2 - base + zl), jnp.where(ends, 3 - zl, 3 - base - zl)
        return jnp.where(i < 2, first, jnp.where(i == 2, low, high))

    def table_copy(i):
        return pltpu.make_async_copy(tbl.at[freq_of(i)], T.at[i], tsem.at[i])

    def cov_copies(i):
        out = []
        for part in range(2):
            for half in range(2):
                rows = pl.ds(pl.multiple_of((k if half == 0 else 1 - k) * ch, ch), ch)
                out.append(pltpu.make_async_copy(
                    cov.at[freq_of(i), part, rows, :],
                    C.at[i, pl.ds(half * ch, ch), pl.ds(part * ch, ch)],
                    csem.at[i, 2 * part + half]))
        return out

    def start_table(i, carry):
        table_copy(i).start()
        return carry

    def start_cov(i, carry):
        for copy in cov_copies(i):
            copy.start()
        return carry

    lax.fori_loop(0, 4, start_table, 0)

    share = slab // n_row
    own = share // n_col
    points = lax.broadcasted_iota(jnp.int32, (table, slab), 0)
    taken = jnp.where(points == idx[...].reshape(1, slab), 1.0, 0.0).astype(BF16)
    lane = lax.broadcasted_iota(jnp.int32, (1, slab), 1)
    source = lane % n_row * share + lane % 128 // n_row * own + lane // 128
    order = jnp.where(lax.broadcasted_iota(jnp.int32, (slab, slab), 0) == source, 1.0, 0.0).astype(BF16)
    OH[...] = jnp.dot(taken, order, preferred_element_type=F32).astype(BF16)

    def chunk(j):
        return pl.ds(pl.multiple_of(j * cr, cr), cr)

    def remote(src, dst, send, recv, to):
        return pltpu.make_async_remote_copy(
            src_ref=src, dst_ref=dst, send_sem=send, recv_sem=recv, device_id=to, device_id_type=MESH)

    to_up = jnp.where(d <= 3, 0, 2)
    to_down = jnp.where((d == 0) | (d >= 6), 0, jnp.where(d == 5, 1, 2))
    from_down = jnp.where(d <= 4, 0, 2)
    from_up = jnp.where(d >= 5, 0, jnp.where(d == 4, 1, 2))

    def send_up(src, j):
        return remote(src, B.at[to_up, chunk(j)], up_send, b_recv.at[to_up, j], up)

    def send_down(src, j):
        return remote(src, B.at[to_down, chunk(j)], dn_send, b_recv.at[to_down, j], down)

    def send_mate(src, j, to=mate):
        return remote(src, B.at[1, chunk(j)], z_send, b_recv.at[1, j], to)

    def send_image(i):
        return remote(IM.at[i, pl.ds(ch, ch)], SI.at[i], s_send.at[i], s_recv.at[i], sib)

    def own_rows(i, j):
        return X.at[i, chunk(j), :]

    def gather(i, carry):
        table_copy(i).wait()
        both = jnp.dot(T[i].reshape(2 * ch, table), OH[...], preferred_element_type=F32)
        na, nb = both[:ch].astype(BF16), both[ch:].astype(BF16)
        X[i, 0:ch, 0:slab] = na
        X[i, 0:ch, slab:2 * slab] = nb
        X[i, ch:2 * ch, 0:slab] = -nb
        X[i, ch:2 * ch, slab:2 * slab] = na

        @pl.when(i == 1)
        def _():
            pl.semaphore_wait(barrier, len(greeted))

        @pl.when(ends & (i == 1))
        def _():
            def go(j, carry):
                send_up(own_rows(0, j), j).start()
                send_down(own_rows(1, j), j).start()
                return carry
            lax.fori_loop(0, NCH, go, 0)

        @pl.when(i == 1)
        def _():
            lax.fori_loop(0, n_slots, start_cov, 0)

        return carry

    lax.fori_loop(0, 4, gather, 0)
    ACC[...] = jnp.zeros_like(ACC)

    def norms(i, carry):
        w = X[i, 0:ch, :].astype(F32)
        squares = jnp.sum((w * w).reshape(ch // 8, 8, 2 * slab), axis=0)
        WT[i] = squares[:, 0:slab] + squares[:, slab:2 * slab]
        return carry

    def image(i, carry):
        for copy in cov_copies(i):
            copy.wait()
        IM[i] = jnp.dot(C[i], X[i], preferred_element_type=F32)
        send_image(i).start()
        return carry

    def wait_in(slot, j):
        remote(B.at[slot, chunk(j)], B.at[slot, chunk(j)], z_send, b_recv.at[slot, j], sib).wait_recv()

    def fold(w, im):
        return jnp.sum((w.astype(F32) * im).reshape(cr // 8, 8, 2 * slab), axis=0)

    def combine(replicas, i, j):
        @pl.when(j == 0)
        def _():
            send_image(i).wait_recv()

        total = IM[i, chunk(j), :] + SI[i, chunk(j), :]
        ACC[i] += fold(replicas[...], total)

    def lines(to, sums):
        line = lax.broadcasted_iota(jnp.int32, (n_col, 128), 0)
        group = lax.broadcasted_iota(jnp.int32, (n_col, 128), 1) // n_row
        out = jnp.zeros((n_col, 128), F32)
        for i in range(4):
            total = jnp.sum(sums(i), axis=0, keepdims=True)
            for m in range(own):
                kept = jnp.where(line == group, total[:, 128 * m:128 * (m + 1)], 0.0)
                for shift in (8, 16, 32, 64):
                    kept += pltpu.roll(kept, shift, 1)
                out = jnp.where(group == own * freq_of(i) + m, kept, out)
        for j in range(n_col):
            to[j] = out[j:j + 1]

    def to_column(src, dst, send, recv):
        for j in sorted(range(1, n_col), key=lambda j: -min(j // 2, 8 - j // 2)):
            to = 2 * mod(y + j // 2, 8) + mod(k + j, 2)
            remote(src.at[to], dst.at[j], send, recv, (r, to, q)).start()

    def column_wait(dst, send, recv):
        others = dst.at[pl.ds(1, n_col - 1)]
        return remote(others, others, send, recv, sib)

    def greet(n):
        for to in near:
            pl.semaphore_signal(gossip.at[n], inc=1, device_id=to, device_id_type=MESH)

    lax.fori_loop(0, n_slots, image, 0)
    lax.fori_loop(0, 4, norms, 0)
    lines(A0, lambda i: WT[i])
    to_column(A0, R0, a0_send, a0_recv)
    greet(0)

    hops = jnp.where(d <= 4, d, 8 - d)

    lag_p = (jnp.where(d <= 4, d, d - 4) - 1) * LAG
    lag_m = (jnp.where(d >= 4, 8 - d, 4 - d) - 1) * LAG
    lag_z = jnp.where(hops == 3, 2 * LAG + 2, hops * LAG)
    lag_0 = jnp.maximum((hops - 1) * LAG, MIN_LAG)
    lag_1 = jnp.maximum(jnp.where(d == 4, 3 * LAG, lag_z), MIN_LAG)
    off = d != 0

    def within(j):
        return (j >= 0) & (j < NCH)

    def step(t, carry):
        jp = t - lag_p

        @pl.when(off & within(jp) & (d != 7))
        def _():
            wait_in(from_down, jp)
            here = B.at[from_down, chunk(jp)]

            @pl.when((d != 4) & (d != 6))
            def _():
                send_up(here, jp).start()

            @pl.when(d >= 5)
            def _():
                send_mate(here, jp).start()

            @pl.when(d == 6)
            def _():
                send_mate(here, jp, up_mate).start()

        jm = t - lag_m

        @pl.when(off & within(jm) & (d != 1))
        def _():
            wait_in(from_up, jm)
            here = B.at[from_up, chunk(jm)]

            @pl.when((d != 4) & (d != 2))
            def _():
                send_down(here, jm).start()

            @pl.when(d <= 3)
            def _():
                send_mate(here, jm).start()

            @pl.when(d == 2)
            def _():
                send_mate(here, jm, down_mate).start()

        jz = t - lag_z

        @pl.when(off & within(jz) & (d != 4))
        def _():
            wait_in(1, jz)

        j0 = t - lag_0

        @pl.when(off & within(j0))
        def _():
            combine(B.at[0, chunk(j0)], 0, j0)

        j1 = t - lag_1

        @pl.when(off & within(j1))
        def _():
            combine(B.at[1, chunk(j1)], 1, j1)

        js = t - MIN_LAG

        @pl.when((d == 0) & within(js))
        def _():
            def each(i, carry):
                combine(own_rows(i, js), i, js)
                return carry
            lax.fori_loop(0, 4, each, 0)

        for n in range(1, ROUNDS):
            @pl.when(t == n * GREET)
            def _():
                pl.semaphore_wait(gossip.at[n - 1], len(near))
                greet(n)

        return carry

    steps = jnp.where(d == 0, MIN_LAG, jnp.maximum(lag_0, lag_1))
    lax.fori_loop(0, NCH + jnp.maximum(steps, (ROUNDS - 1) * GREET + 1 - NCH), step, 0)

    scale = jnp.where(d == 0, 1.0, 2.0).astype(F32)
    lines(A1, lambda i: (ACC[i, :, 0:slab] + ACC[i, :, slab:2 * slab]) * scale)
    to_column(A1, R1, a1_send, a1_recv)
    column_wait(R0, a0_send, a0_recv).wait()
    norm = A0[c]
    for j in range(1, n_col):
        norm += R0[j]
    used = lax.broadcasted_iota(jnp.int32, (1, 128), 1) < 4 * own * n_row
    norm = jnp.where(used, norm, 1.0)

    def sent(ref, sem):
        remote(ref, ref, sem, b_recv.at[0, 0], sib).wait_send()

    whole = B.at[0]

    @pl.when((d != 6) & (d != 7))
    def _():
        sent(whole, up_send)

    @pl.when((d != 2) & (d != 1))
    def _():
        sent(whole, dn_send)

    @pl.when((d == 2) | (d == 3) | (d == 5) | (d == 6))
    def _():
        sent(whole, z_send)

    @pl.when((d == 2) | (d == 6))
    def _():
        sent(whole, z_send)

    def sib_sent(i, carry):
        send_image(i).wait_send()
        return carry

    lax.fori_loop(0, n_slots, sib_sent, 0)

    column_wait(R1, a1_send, a1_recv).wait()
    form = A1[c]
    for j in range(1, n_col):
        form += R1[j]
    power = jnp.where(used, form / norm, 0.0)
    stride = own * n_row
    total = power
    for f in range(1, 4):
        total += pltpu.roll(power, 128 - stride * f, 1)
    A2[...] = jnp.where(used, power, pltpu.roll(total, 4 * stride, 1))
    me = q * n_row + r
    R2[me] = A2[...]
    pl.semaphore_wait(gossip.at[ROUNDS - 1], len(near))

    offsets = [(a, b) for a in range(4) for b in range(8) if a or b]
    for a, b in sorted(offsets, key=lambda p: -min(p[0], 4 - p[0]) - min(p[1], 8 - p[1])):
        at_z = mod(2 * q + zl + b, 8)
        to = (mod(at_z, 2) * 4 + mod(r + a, 4), c, lax.div(at_z, 2))
        remote(A2, R2.at[me], a2_send, a2_recv, to).start()
    others = R2.at[pl.ds(1, n_row * n_freq - 1)]
    remote(others, others, a2_send, a2_recv, sib).wait()
    power = R2[q * n_row]
    for j in range(1, n_row):
        power += R2[q * n_row + j]
    surface = R2[0]
    for j in range(1, n_row * n_freq):
        surface += R2[j]
    mine = mod(128 - r, 128)
    power = pltpu.roll(jnp.broadcast_to(power, (8, 128)), mine, 1)
    surface = pltpu.roll(jnp.broadcast_to(surface, (8, 128)), mine, 1)
    line = lax.broadcasted_iota(jnp.int32, (8, 128), 0)
    lane = lax.broadcasted_iota(jnp.int32, (8, 128), 1)
    out = power
    for f in range(4):
        for m in range(own):
            at = (own * f + m) * n_row - m
            out = jnp.where((line == f) & (lane == m), pltpu.roll(power, (128 - at) % 128, 1), out)
    total = surface
    for m in range(own):
        total = jnp.where(lane == m, pltpu.roll(surface, 128 - 4 * stride - m * n_row + m, 1), total)
    pow_ref[...] = out[0:4, 0:own]
    surf_ref[...] = total[0:1, 0:own] / total_freqs


def solution(mesh):
    n_row, n_col, n_freq = (mesh.shape[a] for a in ("row", "col", "freq"))
    hbm = pl.BlockSpec(memory_space=pltpu.HBM)
    vmem = pl.BlockSpec(memory_space=pltpu.VMEM)

    def local(covariance, replica_table, slab_index):
        freqs, _, ch, table = replica_table.shape
        slab = slab_index.shape[0]
        own = slab // (n_row * n_col)
        sizes = (n_row, n_col, n_freq, ch, slab, table, freqs * n_freq)
        dma = pltpu.SemaphoreType.DMA
        power, surface = pl.pallas_call(
            functools.partial(kernel, sizes),
            out_shape=(jax.ShapeDtypeStruct((freqs, own), F32), jax.ShapeDtypeStruct((1, own), F32)),
            in_specs=[hbm, hbm, vmem],
            out_specs=(vmem, vmem),
            scratch_shapes=[
                pltpu.VMEM((freqs, 2, ch, table), BF16),
                pltpu.VMEM((freqs, 2 * ch, 2 * ch), BF16),
                pltpu.VMEM((freqs, 2 * ch, 2 * slab), BF16),
                pltpu.VMEM((table, slab), BF16),
                pltpu.VMEM((freqs, 2 * ch, 2 * slab), F32),
                pltpu.VMEM((freqs, ch, 2 * slab), F32),
                pltpu.VMEM((3, ch, 2 * slab), BF16),
                pltpu.VMEM((freqs, 8, 2 * slab), F32),
                pltpu.VMEM((freqs, 8, slab), F32),
                pltpu.VMEM((n_col, 1, 128), F32),
                pltpu.VMEM((n_col, 1, 128), F32),
                pltpu.VMEM((n_col, 1, 128), F32),
                pltpu.VMEM((n_col, 1, 128), F32),
                pltpu.VMEM((1, 128), F32),
                pltpu.VMEM((n_row * n_freq, 1, 128), F32),
                dma((4,)), dma((4, 4)), dma((3, NCH)), dma((4,)), dma, dma, dma, dma((4,)),
                dma, dma, dma, dma, dma, dma, pltpu.SemaphoreType.REGULAR((ROUNDS,)),
            ],
            compiler_params=pltpu.CompilerParams(
                collective_id=0, has_side_effects=True, vmem_limit_bytes=210 * 2**18),
        )(covariance, replica_table, slab_index)
        return power, surface.reshape(own)

    in_specs = (P("freq", None, "row", "col"), P("freq", None, "col", None), P())
    out_specs = (P("freq", ("row", "col")), P(("row", "col")))
    return jax.shard_map(local, mesh=mesh, in_specs=in_specs, out_specs=out_specs, check_vma=False)
```
